32 devices in a mesh: dp: 8 (over y, x, core), mp: 4 (over z).
Axes of the slice: x: 2, y: 2, z: 4, core: 2. Of those that a mesh axis runs over, the one named last changes fastest.
Arguments:
- tokens: bfloat16 [11264, 768], P('dp'), may hold values from -6 to 6
- lang: int32 [16], P('dp'), may hold values from 0 to 7
- page_len: int32 [16], P('dp'), may hold values from 374 to 561, as said below
- rel_pos: int32 [16, 704, 704], P('dp', 'mp'), may hold values from 0 to 31, as said below
- rel_x: int32 [16, 704, 704], P('dp', 'mp'), may hold values from 0 to 63, as said below
- rel_y: int32 [16, 704, 704], P('dp', 'mp'), may hold values from 0 to 63, as said below
- lang_table: float32 [8, 768], replicated, may hold values from -3 to 3
- convolution_weight: float32 [3, 768], replicated, may hold values from -2.4 to 2.4
- conv_b: float32 [768], replicated, may hold values from -1.8 to 1.8
- w_qkv: bfloat16 [768, 3, 768], P(None, None, 'mp'), may hold values from -0.21875 to 0.21875
- b_qv: float32 [2, 768], P(None, 'mp'), may hold values from -1.8 to 1.8
- bias_table: float32 [160, 12], replicated, may hold values from -3 to 3
- w_out: bfloat16 [768, 768], P('mp'), may hold values from -1.5 to 1.5
- b_out: float32 [768], replicated, may hold values from -1.8 to 1.8
- ln1_gain: float32 [768], replicated, may hold values from 0.5 to 1.5
- ln1_bias: float32 [768], replicated, may hold values from -1.8 to 1.8
- w_in: bfloat16 [768, 3072], P(None, 'mp'), may hold values from -0.21875 to 0.21875
- b_in: float32 [3072], P('mp'), may hold values from -1.8 to 1.8
- w_down: bfloat16 [3072, 768], P('mp'), may hold values from -0.109375 to 0.109375
- b_down: float32 [768], replicated, may hold values from -1.8 to 1.8
- ln2_gain: float32 [768], replicated, may hold values from 0.5 to 1.5
- ln2_bias: float32 [768], replicated, may hold values from -1.8 to 1.8
- cotangent: bfloat16 [11264, 768], P('dp'), may hold values from -6 to 6
Outputs:
- out: bfloat16 [11264, 768], P('dp')
- d_tokens: bfloat16 [11264, 768], P('dp')
- d_lang_table: float32 [8, 768], replicated
- d_conv_w: float32 [3, 768], replicated
- d_conv_b: float32 [768], replicated
- d_w_qkv: float32 [768, 3, 768], P(None, None, 'mp')
- d_b_qv: float32 [2, 768], P(None, 'mp')
- d_bias_table: float32 [160, 12], replicated
- d_w_out: float32 [768, 768], P('mp')
- d_b_out: float32 [768], replicated
- d_ln1_gain: float32 [768], replicated
- d_ln1_bias: float32 [768], replicated
- d_w_in: float32 [768, 3072], P(None, 'mp')
- d_b_in: float32 [3072], P('mp')
- d_w_down: float32 [3072, 768], P('mp')
- d_b_down: float32 [768], replicated
- d_ln2_gain: float32 [768], replicated
- d_ln2_bias: float32 [768], replicated
The draws below stay inside these ranges and needn't reach their ends.
Inputs may be any that keep to these rules, and one draw needn't show every extreme that they name: `page_len`: the live tokens of a page fill its first slots; one page has exactly 561. `rel_pos`: bucket of the key's reading position minus the query's; positive offsets take the upper 32 // 2 buckets. `rel_x`: bucket of the key's horizontal coordinate minus the query's; positive offsets take the upper 64 // 2 buckets. `rel_y`: bucket of the key's vertical coordinate minus the query's; positive offsets take the upper 64 // 2 buckets.
All inputs are finite; a program needn't handle non-finite values.
Results may differ from the reference program's by a relative error of at most 0.02.
The reference program's roundings to bfloat16 on the way count: a program that leaves them out, or rounds other values in their place, can miss the bound.
Values may be sent and summed in bfloat16 or wider, within the bound.
No kernel may reach another device: no remote copies, remote signals or barrier semaphores. Data moves between devices by JAX's collectives and lax.ppermute only.
A program may use at most 256 MiB of HBM per device.

```python
import math
import jax
import jax.numpy as jnp
from jax import lax

D = 768
H = 12
HD = 64
FF = 3072
NB1 = 32
NB2 = 64
NL = 8
CONV_TAPS = 3
CONV_DILATION = 2
PAGE_SLOTS = 704
PAGE_MAX = 561
PAGES = 16
TOKENS = 11264
N_MP = 4


one_marks = (8, 12, 16, 23, 32, 46, 64, 91)


two_marks = (16, 20, 23, 27, 32, 39, 46, 54, 64, 77, 91, 108, 128, 153, 182, 216)


def bucket_of(offset, half_range, exact_range, mark_list):
    distance = jnp.abs(offset)
    counted = jnp.zeros(distance.shape, jnp.int32)
    for threshold in mark_list:
        counted = counted + (distance >= threshold).astype(jnp.int32)
    far_bucket = exact_range - 1 + counted
    bucket = jnp.where(distance < exact_range, distance, far_bucket)
    return bucket + half_range * (offset > 0).astype(jnp.int32)


def page_layout(page_key):
    reading = jax.random.permutation(jax.random.fold_in(page_key, 1), PAGE_SLOTS).astype(jnp.int32)
    across = jax.random.randint(jax.random.fold_in(page_key, 2), (PAGE_SLOTS,), 0, 1001)
    downward = jax.random.randint(jax.random.fold_in(page_key, 3), (PAGE_SLOTS,), 0, 1001)
    return (reading, across, downward)


def page_keys(key):
    return jax.random.split(jax.random.fold_in(key, 17), PAGES)


def draw_rel_pos(key, part):

    def page_ids(page_key):
        reading = page_layout(page_key)[0]
        return bucket_of(reading[None, :] - reading[:, None], NB1 // 2, 8, one_marks)
    return lax.map(page_ids, page_keys(key))


def draw_rel_x(key, part):

    def page_ids(page_key):
        across = page_layout(page_key)[1]
        return bucket_of(across[None, :] - across[:, None], NB2 // 2, 16, two_marks)
    return lax.map(page_ids, page_keys(key))


def draw_rel_y(key, part):

    def page_ids(page_key):
        downward = page_layout(page_key)[2]
        return bucket_of(downward[None, :] - downward[:, None], NB2 // 2, 16, two_marks)
    return lax.map(page_ids, page_keys(key))


def draw_page_len(key, part):
    shortest = PAGE_MAX * 2 // 3
    lengths = jax.random.randint(jax.random.fold_in(key, 29), (PAGES,), shortest, PAGE_MAX + 1)
    longest = jax.random.randint(jax.random.fold_in(key, 31), (), 0, PAGES)
    page_index = jnp.arange(PAGES, dtype=jnp.int32)
    return jnp.where(page_index == longest, PAGE_MAX, lengths).astype(jnp.int32)


def place_ends(drawn, stream_key, least, high):
    spot = [jax.random.randint(jax.random.fold_in(stream_key, axis), (), 0, length) for axis, length in enumerate(drawn.shape)]
    widest = drawn.shape.index(max(drawn.shape))
    next_to = spot[:widest] + [(spot[widest] + 1) % drawn.shape[widest]] + spot[widest + 1:]
    return drawn.at[tuple(spot)].set(least).at[tuple(next_to)].set(high)


def steps_of(own_key, shape, pieces, smallest, top_value):
    def one(position, parts):
        steps = jax.random.uniform(jax.random.fold_in(jax.random.fold_in(own_key, 6), position), (parts,), jnp.float32, smallest / len(pieces), top_value / len(pieces))
        return jnp.repeat(jnp.exp(steps), shape[position] // parts).reshape((-1,) + (1,) * (len(shape) - position - 1))

    factor_of = one(*pieces[0])
    for cut in pieces[1:]:
        factor_of = factor_of * one(*cut)
    return factor_of


def gaussian(key, extent, deviation, reach, cuts=(), held_as=jnp.bfloat16):
    values = jax.random.normal(key, extent, jnp.float32) * deviation
    if len(cuts) > 0:
        values = steps_of(key, extent, cuts, -0.22, 0.18) * values
    return jnp.clip(values, min=-reach, max=reach).astype(held_as)


def setup_inputs(seed: int = 0) -> dict:
    splits = jax.random.split(jax.random.key(seed), 24)
    tokens = gaussian(splits[0], (TOKENS, D), 1.0, 6.0, ((0, 8),))
    lang = place_ends(jax.random.randint(splits[1], (PAGES,), 0, NL), jax.random.fold_in(splits[1], 1), 0, NL - 1).astype(jnp.int32)
    page_len = draw_page_len(jax.random.fold_in(splits[23], 71), 0)
    rel_pos = draw_rel_pos(jax.random.fold_in(splits[23], 71), 0)
    rel_x = draw_rel_x(jax.random.fold_in(splits[23], 71), 0)
    rel_y = draw_rel_y(jax.random.fold_in(splits[23], 71), 0)
    lang_table = gaussian(splits[6], (NL, D), 0.5, 3.0, (), jnp.float32)
    convolution_weight = gaussian(splits[7], (CONV_TAPS, D), 0.4, 2.4, (), jnp.float32)
    conv_b = gaussian(splits[8], (D,), 0.3, 1.8, (), jnp.float32)
    w_qkv = gaussian(splits[9], (D, 3, D), D ** -0.5, 0.21875, ((2, 4),))
    b_qv = gaussian(splits[10], (2, D), 0.3, 1.8, ((1, 4),), jnp.float32)
    bias_table = gaussian(splits[11], (NB1 + 2 * NB2, H), 0.5, 3.0, (), jnp.float32)
    w_out = gaussian(splits[12], (D, D), 16 ** -0.5, 1.5, ((0, 4),))
    b_out = gaussian(splits[13], (D,), 0.3, 1.8, (), jnp.float32)
    ln1_gain = jnp.clip(1.0 + 0.1 * jax.random.normal(splits[14], (D,), jnp.float32), 0.5, 1.5)
    ln1_bias = gaussian(splits[15], (D,), 0.3, 1.8, (), jnp.float32)
    w_in = gaussian(splits[16], (D, FF), D ** -0.5, 0.21875, ((1, 4),))
    b_in = gaussian(splits[17], (FF,), 0.3, 1.8, ((0, 4),), jnp.float32)
    w_down = gaussian(splits[18], (FF, D), FF ** -0.5, 0.109375, ((0, 4),))
    b_down = gaussian(splits[19], (D,), 0.3, 1.8, (), jnp.float32)
    ln2_gain = jnp.clip(1.0 + 0.1 * jax.random.normal(splits[20], (D,), jnp.float32), 0.5, 1.5)
    ln2_bias = gaussian(splits[21], (D,), 0.3, 1.8, (), jnp.float32)
    cotangent = gaussian(splits[22], (TOKENS, D), 1.0, 6.0, ((0, 8),))
    return dict(tokens=tokens, lang=lang, page_len=page_len, rel_pos=rel_pos, rel_x=rel_x, rel_y=rel_y, lang_table=lang_table, convolution_weight=convolution_weight, conv_b=conv_b, w_qkv=w_qkv, b_qv=b_qv, bias_table=bias_table, w_out=w_out, b_out=b_out, ln1_gain=ln1_gain, ln1_bias=ln1_bias, w_in=w_in, b_in=b_in, w_down=w_down, b_down=b_down, ln2_gain=ln2_gain, ln2_bias=ln2_bias, cotangent=cotangent)


@jax.custom_vjp
def low(v):
    return lax.optimization_barrier(v.astype(jnp.bfloat16)).astype(jnp.float32)

@jax.custom_vjp
def low_back(v):
    return v

def low_keep(v):
    return (low(v), None)

def low_pass(kept, grad):
    return (grad,)

def back_keep(v):
    return (v, None)

def back_low(kept, grad):
    return (low(grad),)
low.defvjp(low_keep, low_pass)
low_back.defvjp(back_keep, back_low)
norm_eps = 1e-05
masked_score = -1000000000.0
highest = lax.Precision.HIGHEST

def layer_norm(inputs, norm_gain, norm_shift):
    row_mean = lax.optimization_barrier(jnp.mean(inputs, axis=-1, keepdims=True))
    centred = inputs - row_mean
    spread = lax.optimization_barrier(jnp.mean(centred * centred, axis=-1, keepdims=True))
    return centred * lax.rsqrt(spread + norm_eps) * norm_gain + norm_shift

def exact_gelu(inputs):
    return jax.nn.gelu(inputs, approximate=False)

def page_group(weights, page_batch):
    lang_table, convolution_weight, conv_b, w_qkv, b_qv, bias_table, w_out, b_out, ln1_gain, ln1_bias, w_in, b_in, w_down, b_down, ln2_gain, ln2_bias = weights
    tok_group, lang_group, length_group, pos_group, x_group, y_group = page_batch
    group_size = tok_group.shape[0]
    group_rows = group_size * PAGE_SLOTS
    slot_index = jnp.arange(PAGE_SLOTS, dtype=jnp.int32)
    live_mask = (slot_index[None, :] < length_group[:, None]).astype(jnp.float32)
    with_lang = tok_group + lang_table[lang_group][:, None, :]
    convolution_reach = CONV_TAPS // 2 * CONV_DILATION
    padded_rows = jnp.pad(with_lang * live_mask[:, :, None], ((0, 0), (convolution_reach, convolution_reach), (0, 0)))
    convolution_sum = conv_b
    for index_of_tap in range(CONV_TAPS):
        convolution_sum = convolution_sum + convolution_weight[index_of_tap] * padded_rows[:, index_of_tap * CONV_DILATION:index_of_tap * CONV_DILATION + PAGE_SLOTS]
    first_in = (with_lang + convolution_sum).reshape(group_rows, D)
    first_low = low(first_in)
    projected = jnp.einsum('rd,dtc->rtc', first_low, w_qkv, precision=highest)
    queries = low(low_back(projected[:, 0] + b_qv[0])).reshape(group_size, PAGE_SLOTS, H, HD)
    key_rows = low(low_back(projected[:, 1])).reshape(group_size, PAGE_SLOTS, H, HD)
    value_rows = low(low_back(projected[:, 2] + b_qv[1])).reshape(group_size, PAGE_SLOTS, H, HD)
    looked_up = bias_table[pos_group] + bias_table[x_group + NB1] + bias_table[y_group + NB1 + NB2]
    head_bias = low(jnp.transpose(looked_up, (0, 3, 1, 2)))
    scores = jnp.einsum('gqhd,gkhd->ghqk', queries, key_rows, precision=highest) * HD ** (-0.5) + head_bias
    scores = low_back(scores)
    scores = jnp.where(live_mask[:, None, None, :] > 0.5, scores, masked_score)
    top_score = lax.optimization_barrier(jnp.max(scores, axis=-1, keepdims=True))
    exp_scores = jnp.exp(scores - top_score)
    probs_full = exp_scores / lax.optimization_barrier(jnp.sum(exp_scores, axis=-1, keepdims=True))
    mixed_heads = jnp.einsum('ghqk,gkhd->gqhd', low(probs_full), value_rows, precision=highest)
    mixed_heads = low(low_back(mixed_heads)).reshape(group_rows, D)
    head_cols = D // N_MP
    attn_sum = jnp.zeros((group_rows, D), jnp.float32)
    for group_index in range(N_MP):
        lo_col = group_index * head_cols
        attn_sum = attn_sum + low(jnp.dot(mixed_heads[:, lo_col:lo_col + head_cols], w_out[lo_col:lo_col + head_cols], precision=highest))
    attn_sum = low_back(attn_sum)
    hidden_one = layer_norm(first_in + attn_sum + b_out, ln1_gain, ln1_bias)
    pre_act = low_back(jnp.dot(low(hidden_one), w_in, precision=highest) + b_in)
    activation = low(exact_gelu(pre_act))
    unit_cols = FF // N_MP
    ffn_sum = jnp.zeros((group_rows, D), jnp.float32)
    for group_index in range(N_MP):
        lo_unit = group_index * unit_cols
        ffn_sum = ffn_sum + low(jnp.dot(activation[:, lo_unit:lo_unit + unit_cols], w_down[lo_unit:lo_unit + unit_cols], precision=highest))
    ffn_sum = low_back(ffn_sum)
    return layer_norm(hidden_one + ffn_sum + b_down, ln2_gain, ln2_bias)

def reference(tokens, lang, page_len, rel_pos, rel_x, rel_y, lang_table, convolution_weight, conv_b, w_qkv, b_qv, bias_table, w_out, b_out, ln1_gain, ln1_bias, w_in, b_in, w_down, b_down, ln2_gain, ln2_bias, cotangent):
    group_size = math.gcd(PAGES, 4)
    group_count = PAGES // group_size

    def forward(tok_all, p_lang, p_convw, p_convb, p_qkv, p_bqv, p_table, p_out, p_bout, p_g1, p_s1, p_in, p_bin, p_down, p_bdown, p_g2, p_s2):
        weights = (p_lang, p_convw, p_convb, p_qkv, p_bqv, p_table, p_out, p_bout, p_g1, p_s1, p_in, p_bin, p_down, p_bdown, p_g2, p_s2)
        page_batch = (tok_all.reshape(group_count, group_size, PAGE_SLOTS, D), lang.reshape(group_count, group_size), page_len.reshape(group_count, group_size), rel_pos.reshape(group_count, group_size, PAGE_SLOTS, PAGE_SLOTS), rel_x.reshape(group_count, group_size, PAGE_SLOTS, PAGE_SLOTS), rel_y.reshape(group_count, group_size, PAGE_SLOTS, PAGE_SLOTS))
        stacked = lax.map(jax.checkpoint(lambda group_batch: page_group(weights, group_batch)), page_batch)
        return stacked.reshape(TOKENS, D)
    result, pullback = jax.vjp(forward, tokens.astype(jnp.float32), lang_table, convolution_weight, conv_b, w_qkv.astype(jnp.float32), b_qv, bias_table, w_out.astype(jnp.float32), b_out, ln1_gain, ln1_bias, w_in.astype(jnp.float32), b_in, w_down.astype(jnp.float32), b_down, ln2_gain, ln2_bias)
    gradients = pullback(cotangent.astype(jnp.float32))
    return (result.astype(jnp.bfloat16), gradients[0].astype(jnp.bfloat16), gradients[1], gradients[2], gradients[3], gradients[4], gradients[5], gradients[6], gradients[7], gradients[8], gradients[9], gradients[10], gradients[11], gradients[12], gradients[13], gradients[14], gradients[15], gradients[16])
```

```python
import functools

import jax
import jax.numpy as jnp
from jax import lax
from jax.experimental import pallas as pl
from jax.experimental.pallas import tpu as pltpu
from jax.sharding import PartitionSpec as P

HD = 64
NB1 = 32
NB2 = 64
CONV_TAPS = 3
CONV_DILATION = 2
PAGE_MAX = 561
LANES = 128
KEYS = -(-PAGE_MAX // LANES) * LANES
CHUNK = 16

norm_eps = 1e-05
masked_score = -1000000000.0
bf16 = jnp.bfloat16
f32 = jnp.float32


def layer_norm(inputs, norm_gain, norm_shift):
    row_mean = jnp.mean(inputs, axis=-1, keepdims=True)
    centred = inputs - row_mean
    spread = jnp.mean(centred * centred, axis=-1, keepdims=True)
    return centred * lax.rsqrt(spread + norm_eps) * norm_gain + norm_shift


def exact_gelu(inputs):
    return jax.nn.gelu(inputs, approximate=False)


def dot_nt(a, b):
    return lax.dot_general(a, b, (((1,), (1,)), ((), ())), preferred_element_type=f32)


def dot_nn(a, b):
    return lax.dot_general(a, b, (((1,), (0,)), ((), ())), preferred_element_type=f32)


def dot_tn(a, b):
    return lax.dot_general(a, b, (((0,), (0,)), ((), ())), preferred_element_type=f32)


def attn_fwd_kernel(len_ref, q_ref, k_ref, v_ref, pos_ref, x_ref, y_ref, tab_ref,
                    mixed_ref, p_ref, s_ref, pb_ref):
    page = pl.program_id(0)
    pair = pl.program_id(1)
    rows = q_ref.shape[0]
    length = len_ref[page]
    lane = lax.broadcasted_iota(jnp.int32, (rows, LANES), 1)
    q = q_ref[...]
    k = k_ref[0]
    v = v_ref[0]
    outs = []
    for sub in range(2):
        mine = (lane >= HD) if sub else (lane < HD)
        s_ref[sub] = dot_nt(jnp.where(mine, q, jnp.zeros_like(q)), k)
        head = pair * 2 + sub
        tabs = [
            jnp.broadcast_to(tab_ref[t, pl.ds(head, 1), :], (CHUNK, LANES)) for t in range(3)
        ]

        def chunk(c, carry, sub=sub, tabs=tabs):
            at = pl.ds(pl.multiple_of(c * CHUNK, CHUNK), CHUNK)
            pieces = []
            for b in range(KEYS // LANES):
                cols = slice(b * LANES, (b + 1) * LANES)
                bias = None
                for tab, ids in zip(tabs, (pos_ref, x_ref, y_ref)):
                    got = jnp.take_along_axis(
                        tab, ids[0, at, cols], axis=1, mode="promise_in_bounds"
                    )
                    bias = got if bias is None else bias + got
                col = lax.broadcasted_iota(jnp.int32, (CHUNK, LANES), 1) + b * LANES
                val = s_ref[sub, at, cols] + bias.astype(bf16).astype(f32)
                pieces.append(jnp.where(col < length, val, masked_score))
            top = functools.reduce(jnp.maximum, pieces)
            top = jnp.max(top, axis=1, keepdims=True)
            es = [jnp.exp(piece - top) for piece in pieces]
            total = jnp.sum(functools.reduce(jnp.add, es), axis=1, keepdims=True)
            inv = 1.0 / total
            for b, e in enumerate(es):
                cols = slice(b * LANES, (b + 1) * LANES)
                prob = e * inv
                p_ref[0, sub, at, cols] = prob
                pb_ref[sub, at, cols] = prob.astype(bf16)
            return carry

        lax.fori_loop(0, rows // CHUNK, chunk, 0, unroll=True)
        outs.append(dot_nn(pb_ref[sub], v))
    mixed_ref[...] = jnp.where(lane < HD, outs[0], outs[1]).astype(bf16)


def attn_bwd_kernel(q_ref, k_ref, v_ref, gm_ref, p_ref, pos_ref, x_ref, y_ref,
                    dq_ref, dk_ref, dv_ref, tab_ref, dp_ref, pb_ref, ds_ref, all_ref):
    page = pl.program_id(0)
    pair = pl.program_id(1)
    rows = q_ref.shape[0]
    heads = 2 * pl.num_programs(1)
    lane = lax.broadcasted_iota(jnp.int32, (rows, LANES), 1)
    q = q_ref[...]
    gm = gm_ref[...]
    k = k_ref[0]
    v = v_ref[0]
    dk = dv = None
    dqs = []
    for sub in range(2):
        mine = (lane >= HD) if sub else (lane < HD)
        qm = jnp.where(mine, q, jnp.zeros_like(q))
        gmm = jnp.where(mine, gm, jnp.zeros_like(gm))
        dp_ref[sub] = dot_nt(gmm, v)
        base = (pair * 2 + sub) * rows

        def chunk(c, carry, sub=sub, base=base):
            at = pl.ds(pl.multiple_of(c * CHUNK, CHUNK), CHUNK)
            to = pl.ds(pl.multiple_of(base + c * CHUNK, CHUNK), CHUNK)
            ps = []
            dps = []
            acc = None
            for b in range(KEYS // LANES):
                cols = slice(b * LANES, (b + 1) * LANES)
                ps.append(p_ref[0, sub, at, cols])
                dps.append(dp_ref[sub, at, cols])
                prod = ps[-1] * dps[-1]
                acc = prod if acc is None else acc + prod
            mean = jnp.sum(acc, axis=1, keepdims=True)
            for b in range(KEYS // LANES):
                cols = slice(b * LANES, (b + 1) * LANES)
                ds = (ps[b] * (dps[b] - mean)).astype(bf16)
                pb_ref[sub, at, cols] = ps[b].astype(bf16)
                ds_ref[sub, at, cols] = ds
                all_ref[b, to, :] = ds.astype(f32)
            return carry

        lax.fori_loop(0, rows // CHUNK, chunk, 0, unroll=True)
        dqs.append(dot_nn(ds_ref[sub], k))
        dkh = dot_tn(ds_ref[sub], qm)
        dvh = dot_tn(pb_ref[sub], gmm)
        dk = dkh if dk is None else dk + dkh
        dv = dvh if dv is None else dv + dvh
    dq_ref[...] = (jnp.where(lane < HD, dqs[0], dqs[1]) * HD ** -0.5).astype(bf16)
    dk_ref[0] = dk.astype(bf16)
    dv_ref[0] = dv.astype(bf16)

    @pl.when((page == 0) & (pair == 0))
    def _():
        tab_ref[...] = jnp.zeros_like(tab_ref)

    @pl.when(pair == pl.num_programs(1) - 1)
    def _():
        nheads = tab_ref.shape[1]

        def row(i, accs):
            g = jnp.concatenate(
                [all_ref[b, pl.ds(i, nheads, stride=rows), :] for b in range(KEYS // LANES)],
                axis=1,
            ).astype(bf16)
            new = []
            for acc, ids, count in zip(accs, (pos_ref, x_ref, y_ref), (NB1, NB2, NB2)):
                idr = ids[0, pl.ds(i, 1), :].astype(f32).astype(bf16)
                bucket = lax.broadcasted_iota(jnp.int32, (count, KEYS), 0).astype(f32).astype(bf16)
                hit = jnp.where(bucket == idr, jnp.ones((), bf16), jnp.zeros((), bf16))
                new.append(acc + dot_nt(hit, g))
            return tuple(new)

        accs = tuple(jnp.zeros((c, nheads), f32) for c in (NB1, NB2, NB2))
        accs = lax.fori_loop(0, rows, row, accs, unroll=4)
        tab_ref[0:NB1, :] += accs[0]
        tab_ref[NB1 : NB1 + NB2, :] += accs[1]
        tab_ref[NB1 + NB2 : NB1 + 2 * NB2, :] += accs[2]


def attn_specs(rows):
    qs = pl.BlockSpec((rows, LANES), lambda p, h, *_: (p, h))
    ks = pl.BlockSpec((1, KEYS, LANES), lambda p, h, *_: (p, 0, h))
    ids = pl.BlockSpec((1, rows, KEYS), lambda p, h, *_: (p, 0, 0))
    ps = pl.BlockSpec((1, 2, rows, KEYS), lambda p, h, *_: (p, h, 0, 0))
    return qs, ks, ids, ps


def attn_fwd(page_len, q, k, v, pos, x, y, tab):
    pages, rows, _ = pos.shape
    heads = q.shape[1] // HD
    qs, ks, ids, ps = attn_specs(rows)
    return pl.pallas_call(
        attn_fwd_kernel,
        out_shape=(
            jax.ShapeDtypeStruct(q.shape, bf16),
            jax.ShapeDtypeStruct((pages, heads, rows, KEYS), f32),
        ),
        grid_spec=pltpu.PrefetchScalarGridSpec(
            num_scalar_prefetch=1,
            grid=(pages, heads // 2),
            in_specs=[qs, ks, ks, ids, ids, ids,
                      pl.BlockSpec(tab.shape, lambda p, h, *_: (0, 0, 0))],
            out_specs=(qs, ps),
            scratch_shapes=[pltpu.VMEM((2, rows, KEYS), f32), pltpu.VMEM((2, rows, KEYS), bf16)],
        ),
    )(page_len, q, k, v, pos, x, y, tab)


def attn_bwd(q, k, v, gm, p, pos, x, y):
    pages, rows, _ = pos.shape
    heads = q.shape[1] // HD
    qs, ks, ids, ps = attn_specs(rows)
    kv = jax.ShapeDtypeStruct(k.shape, bf16)
    return pl.pallas_call(
        attn_bwd_kernel,
        out_shape=(
            jax.ShapeDtypeStruct(q.shape, bf16), kv, kv,
            jax.ShapeDtypeStruct((NB1 + 2 * NB2, heads), f32),
        ),
        grid=(pages, heads // 2),
        in_specs=[qs, ks, ks, qs, ps, ids, ids, ids],
        out_specs=(qs, ks, ks, pl.BlockSpec((NB1 + 2 * NB2, heads), lambda p, h: (0, 0))),
        scratch_shapes=[
            pltpu.VMEM((2, rows, KEYS), f32),
            pltpu.VMEM((2, rows, KEYS), bf16),
            pltpu.VMEM((2, rows, KEYS), bf16),
            pltpu.VMEM((KEYS // LANES, heads * rows, LANES), f32),
        ],
    )(q, k, v, gm, p, pos, x, y)


def body(tokens, lang, page_len, rel_pos, rel_x, rel_y, lang_table, convolution_weight, conv_b,
         w_qkv, b_qv, bias_table, w_out, b_out, ln1_gain, ln1_bias, w_in, b_in, w_down, b_down,
         ln2_gain, ln2_bias, cotangent, *, n_dp, n_mp):
    dp = lax.axis_index("dp")
    mp = lax.axis_index("mp")
    page_count = page_len.shape[0]
    rows = rel_pos.shape[1]
    slots = rel_pos.shape[2]
    width = tokens.shape[1]
    cols = w_qkv.shape[2]
    units = w_in.shape[1]
    own_rows = page_count * rows
    score_scale = HD ** (-0.5)

    def share(w):
        step = w.shape[0] // n_dp
        return lax.dynamic_slice_in_dim(w, dp * step, step, 0)

    in_all = lax.all_gather(share(w_in), ("mp", "dp"), axis=0, tiled=True)
    down_all = lax.all_gather(share(w_down), ("mp", "dp"), axis=0, tiled=True)
    in_all = in_all.reshape(n_mp, width, units)
    down_all = down_all.reshape(n_mp, units, width)

    def spread(block, paired):
        half = block.shape[0] // 2
        odd = dp % 2
        sent = lax.dynamic_slice_in_dim(block, odd * half, half, 0) if paired else block
        got = [
            lax.ppermute(sent, "mp", [(i, (i + s) % n_mp) for i in range(n_mp)])
            for s in range(1, n_mp)
        ]
        if paired:
            mate = [(i, i ^ 1) for i in range(n_dp)]
            other = [lax.ppermute(g, "dp", mate) for g in got]
            got = [
                jnp.concatenate([jnp.where(odd == 0, g, o), jnp.where(odd == 0, o, g)], axis=0)
                for g, o in zip(got, other)
            ]
        line = jnp.stack([block] + got)
        order = (mp - jnp.arange(n_mp)) % n_mp
        return jnp.take(line, order, axis=0, mode="clip")

    qkv_t = jnp.transpose(w_qkv.reshape(width, 3 * cols))
    paired = n_dp % 2 == 0
    attn_w = spread(jnp.concatenate([qkv_t, w_out], axis=0), paired)
    wq_t, wk_t, wv_t, wo = [
        attn_w[:, t * cols : (t + 1) * cols].reshape(n_mp * cols, width) for t in range(4)
    ]
    small = spread(jnp.concatenate([b_in, b_qv.reshape(-1)]).reshape(-1, LANES), False)
    small = small.reshape(n_mp, units + 2 * cols)
    bin_all = small[:, :units]
    bq = small[:, units : units + cols].reshape(-1)
    bv = small[:, units + cols :].reshape(-1)

    slot_index = lax.broadcasted_iota(jnp.int32, (page_count, slots), 1)
    live_rows = (slot_index < page_len[:, None]).astype(f32)[:, :, None]
    languages = lax.broadcasted_iota(jnp.int32, (1, lang_table.shape[0]), 1)
    lang_pick = (lang[:, None] == languages).astype(f32)
    convolution_reach = CONV_TAPS // 2 * CONV_DILATION

    def embed(tok_in, lang_weights, kernel_taps, kernel_bias):
        with_lang = (
            tok_in + jnp.dot(lang_pick, lang_weights, precision=lax.Precision.HIGHEST)[:, None, :]
        )
        padded_rows = jnp.pad(
            with_lang * live_rows, ((0, 0), (convolution_reach, convolution_reach), (0, 0))
        )
        convolution_sum = kernel_bias
        for index_of_tap in range(CONV_TAPS):
            convolution_sum = (
                convolution_sum
                + kernel_taps[index_of_tap]
                * padded_rows[
                    :, index_of_tap * CONV_DILATION : index_of_tap * CONV_DILATION + slots
                ]
            )
        return with_lang + convolution_sum

    def own(a):
        return lax.dynamic_slice_in_dim(a, mp * rows, rows, 1).reshape(own_rows, a.shape[2])

    tok_in = tokens.astype(f32).reshape(page_count, slots, width)
    first_pages, embed_back = jax.vjp(embed, tok_in, lang_table, convolution_weight, conv_b)
    first_own = own(first_pages)
    first_own_low = first_own.astype(bf16)
    first_keys = first_pages[:, :KEYS].astype(bf16).reshape(page_count * KEYS, width)
    queries = ((dot_nt(first_own_low, wq_t) + bq).astype(bf16) * score_scale).astype(bf16)
    key_rows = dot_nt(first_keys, wk_t).astype(bf16).reshape(page_count, KEYS, width)
    value_rows = (dot_nt(first_keys, wv_t) + bv).astype(bf16).reshape(page_count, KEYS, width)
    table_t = jnp.transpose(bias_table)
    tab = jnp.stack([
        jnp.pad(t, ((0, 0), (0, LANES - t.shape[1])))
        for t in (table_t[:, :NB1], table_t[:, NB1 : NB1 + NB2], table_t[:, NB1 + NB2 :])
    ])
    mixed_low, probs = attn_fwd(page_len, queries, key_rows, value_rows, rel_pos, rel_x, rel_y, tab)
    attn_sum = 0.0
    for g in range(n_mp):
        part = dot_nn(mixed_low[:, g * cols : (g + 1) * cols], wo[g * cols : (g + 1) * cols])
        attn_sum = attn_sum + part.astype(bf16).astype(f32)
    resid_one = first_own + attn_sum + b_out
    hidden_one, norm_one_back = jax.vjp(layer_norm, resid_one, ln1_gain, ln1_bias)
    hidden_low = hidden_one.astype(bf16)
    ffn_sum = 0.0
    acts = []
    for g in range(n_mp):
        pre_act = dot_nn(hidden_low, in_all[g]) + bin_all[g]
        activation, gelu_back = jax.vjp(exact_gelu, pre_act)
        activ_low = activation.astype(bf16)
        acts.append((activ_low, gelu_back))
        ffn_sum = ffn_sum + dot_nn(activ_low, down_all[g]).astype(bf16).astype(f32)
    resid_two = hidden_one + ffn_sum + b_down
    result, norm_two_back = jax.vjp(layer_norm, resid_two, ln2_gain, ln2_bias)
    out_own = result.astype(bf16).reshape(page_count, rows, width)

    cot_own = own(cotangent.reshape(page_count, slots, width)).astype(f32)
    grad_two, d_ln2_gain, d_ln2_bias = norm_two_back(cot_own)
    d_b_down = jnp.sum(grad_two, axis=0)
    grad_ffn = grad_two.astype(bf16)
    grad_hidden = grad_two
    d_in = []
    d_down = []
    d_bin = []
    for g in range(n_mp):
        activ_low, gelu_back = acts[g]
        d_down.append(dot_tn(activ_low, grad_ffn).astype(bf16))
        grad_pre = gelu_back(dot_nt(grad_ffn, down_all[g]))[0].astype(bf16)
        d_in.append(dot_tn(hidden_low, grad_pre).astype(bf16))
        d_bin.append(jnp.sum(grad_pre.astype(f32), axis=0))
        grad_hidden = grad_hidden + dot_nt(grad_pre, in_all[g])
    grad_one, d_ln1_gain, d_ln1_bias = norm_one_back(grad_hidden)
    d_b_out = jnp.sum(grad_one, axis=0)
    grad_attn = grad_one.astype(bf16)
    grad_mixed = dot_nt(grad_attn, wo).astype(bf16)
    d_queries, d_keys, d_values, table_part = attn_bwd(
        queries, key_rows, value_rows, grad_mixed, probs, rel_pos, rel_x, rel_y
    )
    dk_flat = d_keys.reshape(page_count * KEYS, width)
    dv_flat = d_values.reshape(page_count * KEYS, width)

    own_part = (grad_one + dot_nn(d_queries, wq_t)).reshape(page_count, rows, width)
    key_part = (dot_nn(dk_flat, wk_t) + dot_nn(dv_flat, wv_t)).reshape(page_count, KEYS, width)
    grad_first = jnp.pad(key_part, ((0, 0), (0, slots - KEYS), (0, 0)))
    grad_first = lax.dynamic_update_slice_in_dim(
        grad_first,
        lax.dynamic_slice_in_dim(grad_first, mp * rows, rows, 1) + own_part,
        mp * rows,
        1,
    )
    d_tokens, d_lang_table, d_conv_w, d_conv_b = embed_back(grad_first)
    d_tokens = lax.psum(d_tokens.astype(bf16), "mp")

    out = lax.all_gather(out_own, "mp", axis=1, tiled=True)

    ffn_parts = jnp.concatenate(
        [jnp.stack(d_in), jnp.stack(d_down)], axis=0
    ).reshape(2 * n_mp, n_dp, width // n_dp, units)
    attn_parts = jnp.stack([
        dot_tn(first_own_low, d_queries).astype(bf16),
        dot_tn(first_keys, dk_flat).astype(bf16),
        dot_tn(first_keys, dv_flat).astype(bf16),
        dot_tn(grad_attn, mixed_low).astype(bf16),
    ]).reshape(4, n_dp, width // n_dp, n_mp * cols)
    ffn_parts = jnp.transpose(ffn_parts, (1, 0, 2, 3))
    attn_parts = jnp.transpose(attn_parts, (1, 0, 2, 3))
    ffn_parts = lax.psum_scatter(ffn_parts, "dp", scatter_dimension=0, tiled=False)
    attn_parts = lax.psum_scatter(attn_parts, "dp", scatter_dimension=0, tiled=False)
    ffn_parts = ffn_parts.reshape(2, n_mp, width // n_dp, units)
    ffn_parts = jnp.transpose(ffn_parts, (1, 0, 2, 3)).reshape(n_mp, -1, LANES)
    attn_parts = attn_parts.reshape(4 * (width // n_dp), n_mp, cols)
    attn_parts = jnp.transpose(attn_parts, (1, 0, 2)).reshape(n_mp, -1, LANES)
    split = ffn_parts.shape[1]
    shares = lax.psum_scatter(
        jnp.concatenate([ffn_parts, attn_parts], axis=1), "mp", scatter_dimension=0, tiled=False
    )
    blocks = lax.all_gather(shares, "dp", axis=0, tiled=False).astype(f32)
    ffn_blocks = blocks[:, :split].reshape(n_dp, 2, width // n_dp, units)
    d_w_in, d_w_down = [ffn_blocks[:, t].reshape(width, units) for t in range(2)]
    attn_blocks = blocks[:, split:].reshape(n_dp, 4, width // n_dp, cols)
    attn_blocks = jnp.transpose(attn_blocks, (1, 0, 2, 3)).reshape(4, width, cols)
    d_w_qkv = jnp.transpose(attn_blocks[:3], (1, 0, 2))
    d_w_out = jnp.transpose(attn_blocks[3])

    dq_sum = jnp.sum(d_queries.astype(f32), axis=0)
    dv_sum = jnp.sum(dv_flat.astype(f32), axis=0)
    smalls = [
        d_lang_table, d_conv_w, d_conv_b, dq_sum, dv_sum, table_part, d_b_out, d_ln1_gain,
        d_ln1_bias, jnp.concatenate(d_bin), d_b_down, d_ln2_gain, d_ln2_bias,
    ]
    flat = lax.psum(jnp.concatenate([s.reshape(-1) for s in smalls]), ("dp", "mp"))
    back = []
    start = 0
    for s in smalls:
        back.append(flat[start : start + s.size].reshape(s.shape))
        start += s.size
    (d_lang_table, d_conv_w, d_conv_b, dq_sum, dv_sum, d_bias_table, d_b_out, d_ln1_gain,
     d_ln1_bias, d_b_in, d_b_down, d_ln2_gain, d_ln2_bias) = back
    d_b_qv = jnp.stack([
        lax.dynamic_slice_in_dim(dq_sum, mp * cols, cols),
        lax.dynamic_slice_in_dim(dv_sum, mp * cols, cols),
    ])
    d_b_in = lax.dynamic_slice_in_dim(d_b_in, mp * units, units)
    return (
        out.reshape(page_count * slots, width),
        d_tokens.reshape(page_count * slots, width),
        d_lang_table, d_conv_w, d_conv_b, d_w_qkv, d_b_qv, d_bias_table, d_w_out, d_b_out,
        d_ln1_gain, d_ln1_bias, d_w_in, d_b_in, d_w_down, d_b_down, d_ln2_gain, d_ln2_bias,
    )


def solution(mesh):
    in_specs = (
        P("dp", None), P("dp"), P("dp"),
        P("dp", "mp", None), P("dp", "mp", None), P("dp", "mp", None),
        P(), P(), P(), P(None, None, "mp"), P(None, "mp"), P(), P("mp", None),
        P(), P(), P(), P(None, "mp"), P("mp"), P("mp", None), P(), P(), P(), P("dp", None),
    )
    out_specs = (
        P("dp", None), P("dp", None), P(), P(), P(), P(None, None, "mp"), P(None, "mp"), P(),
        P("mp", None), P(), P(), P(), P(None, "mp"), P("mp"), P("mp", None), P(), P(), P(),
    )
    step = functools.partial(body, n_dp=mesh.shape["dp"], n_mp=mesh.shape["mp"])
    return jax.shard_map(step, mesh=mesh, in_specs=in_specs, out_specs=out_specs, check_vma=False)
```

```python
import functools

import jax
import jax.numpy as jnp
from jax import lax
from jax.experimental import pallas as pl
from jax.experimental.pallas import tpu as pltpu
from jax.sharding import PartitionSpec as P

HD = 64
NB1 = 32
NB2 = 64
CONV_TAPS = 3
CONV_DILATION = 2
PAGE_MAX = 561
LANES = 128
KEYS = -(-PAGE_MAX // LANES) * LANES
CHUNK = 16

norm_eps = 1e-05
masked_score = -1000000000.0
bf16 = jnp.bfloat16
f32 = jnp.float32


def layer_norm(inputs, norm_gain, norm_shift):
    row_mean = jnp.mean(inputs, axis=-1, keepdims=True)
    centred = inputs - row_mean
    spread = jnp.mean(centred * centred, axis=-1, keepdims=True)
    return centred * lax.rsqrt(spread + norm_eps) * norm_gain + norm_shift


def exact_gelu(inputs):
    return jax.nn.gelu(inputs, approximate=False)


def dot_nt(a, b):
    return lax.dot_general(a, b, (((1,), (1,)), ((), ())), preferred_element_type=f32)


def dot_nn(a, b):
    return lax.dot_general(a, b, (((1,), (0,)), ((), ())), preferred_element_type=f32)


def dot_tn(a, b):
    return lax.dot_general(a, b, (((0,), (0,)), ((), ())), preferred_element_type=f32)


def attn_fwd_kernel(len_ref, own_ref, all_ref, one_ref, two_ref, bias_ref, pos_ref, x_ref, y_ref,
                    tab_ref, *rest):
    mixed_ref, p_ref, q_ref, k_ref, v_ref, s_ref, pb_ref = rest[-7:]
    page = pl.program_id(0)
    rows, width = q_ref.shape[1:]
    length = len_ref[page]
    lane = lax.broadcasted_iota(jnp.int32, (rows, width), 1)
    q = (dot_nt(own_ref[...], one_ref[0:width, :]) + bias_ref[0:1, :]).astype(bf16)
    q_ref[0] = (q.astype(f32) * HD ** -0.5).astype(bf16)
    k_ref[0, 0] = dot_nt(all_ref[...], one_ref[width : 2 * width, :]).astype(bf16)
    v_ref[0, 0] = (dot_nt(all_ref[...], two_ref[0:width, :]) + bias_ref[1:2, :]).astype(bf16)
    q = q_ref[0]
    k = k_ref[0, 0]
    v = v_ref[0, 0]
    mixed = jnp.zeros((rows, width), f32)
    for sub in range(width // HD):
        mine = (lane >= sub * HD) & (lane < (sub + 1) * HD)
        s_ref[sub] = dot_nt(jnp.where(mine, q, jnp.zeros_like(q)), k)
        tabs = [
            jnp.broadcast_to(tab_ref[t, sub : sub + 1, :], (CHUNK, LANES)) for t in range(3)
        ]

        def chunk(c, carry, sub=sub, tabs=tabs):
            at = pl.ds(pl.multiple_of(c * CHUNK, CHUNK), CHUNK)
            pieces = []
            for b in range(KEYS // LANES):
                cols = slice(b * LANES, (b + 1) * LANES)
                bias = None
                for tab, ids in zip(tabs, (pos_ref, x_ref, y_ref)):
                    got = jnp.take_along_axis(
                        tab, ids[0, at, cols], axis=1, mode="promise_in_bounds"
                    )
                    bias = got if bias is None else bias + got
                col = lax.broadcasted_iota(jnp.int32, (CHUNK, LANES), 1) + b * LANES
                val = s_ref[sub, at, cols] + bias.astype(bf16).astype(f32)
                pieces.append(jnp.where(col < length, val, masked_score))
            top = functools.reduce(jnp.maximum, pieces)
            top = jnp.max(top, axis=1, keepdims=True)
            es = [jnp.exp(piece - top) for piece in pieces]
            total = jnp.sum(functools.reduce(jnp.add, es), axis=1, keepdims=True)
            inv = 1.0 / total
            for b, e in enumerate(es):
                cols = slice(b * LANES, (b + 1) * LANES)
                prob = e * inv
                p_ref[0, 0, sub, at, cols] = prob
                pb_ref[sub, at, cols] = prob.astype(bf16)
            return carry

        lax.fori_loop(0, rows // CHUNK, chunk, 0, unroll=True)
        mixed = jnp.where(mine, dot_nn(pb_ref[sub], v), mixed)
    mixed_ref[0] = mixed.astype(bf16)


def attn_bwd_kernel(q_ref, k_ref, v_ref, gm_ref, p_ref, pos_ref, x_ref, y_ref,
                    dq_ref, dk_ref, dv_ref, tab_ref, dp_ref, pb_ref, ds_ref, all_ref):
    page = pl.program_id(0)
    group = pl.program_id(1)
    rows, width = q_ref.shape[1:]
    heads = width // HD
    lane = lax.broadcasted_iota(jnp.int32, (rows, width), 1)
    q = q_ref[0]
    gm = gm_ref[0]
    k = k_ref[0, 0]
    v = v_ref[0, 0]
    dk = dv = None
    dq = jnp.zeros((rows, width), f32)
    for sub in range(heads):
        mine = (lane >= sub * HD) & (lane < (sub + 1) * HD)
        qm = jnp.where(mine, q, jnp.zeros_like(q))
        gmm = jnp.where(mine, gm, jnp.zeros_like(gm))
        dp_ref[sub] = dot_nt(gmm, v)
        base = (group * heads + sub) * rows

        def chunk(c, carry, sub=sub, base=base):
            at = pl.ds(pl.multiple_of(c * CHUNK, CHUNK), CHUNK)
            to = pl.ds(pl.multiple_of(base + c * CHUNK, CHUNK), CHUNK)
            ps = []
            dps = []
            acc = None
            for b in range(KEYS // LANES):
                cols = slice(b * LANES, (b + 1) * LANES)
                ps.append(p_ref[0, 0, sub, at, cols])
                dps.append(dp_ref[sub, at, cols])
                prod = ps[-1] * dps[-1]
                acc = prod if acc is None else acc + prod
            mean = jnp.sum(acc, axis=1, keepdims=True)
            for b in range(KEYS // LANES):
                cols = slice(b * LANES, (b + 1) * LANES)
                ds = (ps[b] * (dps[b] - mean)).astype(bf16)
                pb_ref[sub, at, cols] = ps[b].astype(bf16)
                ds_ref[sub, at, cols] = ds
                all_ref[b, to, :] = ds.astype(f32)
            return carry

        lax.fori_loop(0, rows // CHUNK, chunk, 0, unroll=True)
        dq = jnp.where(mine, dot_nn(ds_ref[sub], k), dq)
        dkh = dot_tn(ds_ref[sub], qm)
        dvh = dot_tn(pb_ref[sub], gmm)
        dk = dkh if dk is None else dk + dkh
        dv = dvh if dv is None else dv + dvh
    dq_ref[0] = (dq * HD ** -0.5).astype(bf16)
    dk_ref[0, 0] = dk.astype(bf16)
    dv_ref[0, 0] = dv.astype(bf16)

    @pl.when((page == 0) & (group == 0))
    def _():
        tab_ref[...] = jnp.zeros_like(tab_ref)

    @pl.when(group == pl.num_programs(1) - 1)
    def _():
        nheads = tab_ref.shape[1]

        def row(i, accs):
            g = jnp.concatenate(
                [all_ref[b, pl.ds(i, nheads, stride=rows), :] for b in range(KEYS // LANES)],
                axis=1,
            ).astype(bf16)
            new = []
            for acc, ids, count in zip(accs, (pos_ref, x_ref, y_ref), (NB1, NB2, NB2)):
                idr = ids[0, pl.ds(i, 1), :].astype(f32).astype(bf16)
                bucket = lax.broadcasted_iota(jnp.int32, (count, KEYS), 0).astype(f32).astype(bf16)
                hit = jnp.where(bucket == idr, jnp.ones((), bf16), jnp.zeros((), bf16))
                new.append(acc + dot_nt(hit, g))
            return tuple(new)

        accs = tuple(jnp.zeros((c, nheads), f32) for c in (NB1, NB2, NB2))
        accs = lax.fori_loop(0, rows, row, accs, unroll=4)
        tab_ref[0:NB1, :] += accs[0]
        tab_ref[NB1 : NB1 + NB2, :] += accs[1]
        tab_ref[NB1 + NB2 : NB1 + 2 * NB2, :] += accs[2]


def attn_fwd(group, groups, page_len, own_in, all_in, one, two, bias, pos, x, y, tab, held):
    pages, rows, _ = pos.shape
    width = bias.shape[1]
    depth = own_in.shape[1]
    heads = width // HD
    ids = pl.BlockSpec((1, rows, KEYS), lambda p, *_: (p, 0, 0))
    kv = pl.BlockSpec((1, 1, KEYS, width), lambda p, *_: (group, p, 0, 0))
    qs = pl.BlockSpec((1, rows, width), lambda p, *_: (group, p, 0))
    kv_all = jax.ShapeDtypeStruct((groups, pages, KEYS, width), bf16)
    q_all = jax.ShapeDtypeStruct((groups, pages * rows, width), bf16)
    carried = [pl.BlockSpec(memory_space=pl.ANY)] * len(held)
    elements = pages * rows * heads * KEYS
    return pl.pallas_call(
        attn_fwd_kernel,
        out_shape=(
            q_all,
            jax.ShapeDtypeStruct((groups, pages, heads, rows, KEYS), f32),
            q_all,
            kv_all,
            kv_all,
        ),
        grid_spec=pltpu.PrefetchScalarGridSpec(
            num_scalar_prefetch=1,
            grid=(pages,),
            in_specs=[
                pl.BlockSpec((rows, depth), lambda p, *_: (p, 0)),
                pl.BlockSpec((KEYS, depth), lambda p, *_: (p, 0)),
                pl.BlockSpec(one.shape, lambda p, *_: (0, 0)),
                pl.BlockSpec(two.shape, lambda p, *_: (0, 0)),
                pl.BlockSpec(bias.shape, lambda p, *_: (0, 0)),
                ids, ids, ids,
                pl.BlockSpec(tab.shape, lambda p, *_: (0, 0, 0)),
            ] + carried,
            out_specs=(
                qs,
                pl.BlockSpec((1, 1, heads, rows, KEYS), lambda p, *_: (group, p, 0, 0, 0)),
                qs, kv, kv,
            ),
            scratch_shapes=[
                pltpu.VMEM((heads, rows, KEYS), f32), pltpu.VMEM((heads, rows, KEYS), bf16)
            ],
        ),
        input_output_aliases={10 + i: i for i in range(len(held))},
        cost_estimate=pl.CostEstimate(
            flops=20000 * elements, transcendentals=elements, bytes_accessed=16 * elements
        ),
    )(page_len, own_in, all_in, one, two, bias, pos, x, y, tab, *held)


def attn_bwd(q, k, v, gm, p, pos, x, y):
    pages, rows, _ = pos.shape
    groups, _, width = q.shape
    heads = width // HD
    qs = pl.BlockSpec((1, rows, width), lambda p, g: (g, p, 0))
    ks = pl.BlockSpec((1, 1, KEYS, width), lambda p, g: (g, p, 0, 0))
    ids = pl.BlockSpec((1, rows, KEYS), lambda p, g: (p, 0, 0))
    ps = pl.BlockSpec((1, 1, heads, rows, KEYS), lambda p, g: (g, p, 0, 0, 0))
    kv = jax.ShapeDtypeStruct(k.shape, bf16)
    table = (NB1 + 2 * NB2, groups * heads)
    elements = pages * rows * groups * heads * KEYS
    return pl.pallas_call(
        attn_bwd_kernel,
        out_shape=(jax.ShapeDtypeStruct(q.shape, bf16), kv, kv, jax.ShapeDtypeStruct(table, f32)),
        grid=(pages, groups),
        in_specs=[qs, ks, ks, qs, ps, ids, ids, ids],
        out_specs=(qs, ks, ks, pl.BlockSpec(table, lambda p, g: (0, 0))),
        scratch_shapes=[
            pltpu.VMEM((heads, rows, KEYS), f32),
            pltpu.VMEM((heads, rows, KEYS), bf16),
            pltpu.VMEM((heads, rows, KEYS), bf16),
            pltpu.VMEM((KEYS // LANES, groups * heads * rows, LANES), f32),
        ],
        cost_estimate=pl.CostEstimate(
            flops=20000 * elements, transcendentals=elements, bytes_accessed=16 * elements
        ),
    )(q, k, v, gm, p, pos, x, y)


def body(tokens, lang, page_len, rel_pos, rel_x, rel_y, lang_table, convolution_weight, conv_b,
         w_qkv, b_qv, bias_table, w_out, b_out, ln1_gain, ln1_bias, w_in, b_in, w_down, b_down,
         ln2_gain, ln2_bias, cotangent, *, n_dp, n_mp):
    dp = lax.axis_index("dp")
    mp = lax.axis_index("mp")
    page_count = page_len.shape[0]
    rows = rel_pos.shape[1]
    slots = rel_pos.shape[2]
    width = tokens.shape[1]
    cols = w_qkv.shape[2]
    units = w_in.shape[1]
    own_rows = page_count * rows
    heads_here = cols // HD
    score_scale = HD ** (-0.5)
    paired = n_dp % 2 == 0
    order = (mp - jnp.arange(n_mp)) % n_mp

    def turned(a, axis=0):
        return jnp.take(a, order, axis=axis, mode="clip")

    def shift(a, s):
        return lax.ppermute(a, "mp", [(i, (i + s) % n_mp) for i in range(n_mp)])

    step = width // n_dp
    unit_step = units // n_dp
    share = jnp.concatenate([
        lax.dynamic_slice_in_dim(w_in, dp * step, step, 0),
        lax.dynamic_slice_in_dim(w_down, dp * unit_step, unit_step, 0),
    ], axis=1)
    ffn_all = lax.all_gather(share, ("mp", "dp"), axis=0, tiled=True)
    ffn_all = ffn_all.reshape(n_mp, width, 2 * units)
    in_all = [ffn_all[g, :, :units] for g in range(n_mp)]
    down_all = [ffn_all[g, :, units:] for g in range(n_mp)]

    biases = jnp.concatenate([b_in, b_qv.reshape(-1)])
    thirds = []
    for _ in range(3):
        top = lax.reduce_precision(biases, 8, 7)
        thirds.append(top.astype(bf16))
        biases = biases - top
    thirds = jnp.concatenate(thirds)
    tail = -(-thirds.size // (16 * width)) * 16
    thirds = jnp.pad(thirds, (0, tail * width - thirds.size)).reshape(tail, width)
    qkv_t = jnp.transpose(w_qkv.reshape(width, 3 * cols))
    halves = [
        jnp.concatenate([qkv_t[: 2 * cols], thirds[: tail // 2]], axis=0),
        jnp.concatenate([qkv_t[2 * cols :], w_out, thirds[tail // 2 :]], axis=0),
    ]
    odd = dp % 2
    if paired:
        moving = jnp.where(odd == 0, halves[0], halves[1])
        moved = [shift(moving, s) for s in range(1, n_mp)]
    else:
        moved = [shift(jnp.stack(halves), s) for s in range(1, n_mp)]

    slot_index = lax.broadcasted_iota(jnp.int32, (page_count, slots), 1)
    live_rows = (slot_index < page_len[:, None]).astype(f32)[:, :, None]
    languages = lax.broadcasted_iota(jnp.int32, (1, lang_table.shape[0]), 1)
    lang_pick = (lang[:, None] == languages).astype(f32)
    convolution_reach = CONV_TAPS // 2 * CONV_DILATION

    def embed(tok_in, lang_weights, kernel_taps, kernel_bias):
        with_lang = (
            tok_in + jnp.dot(lang_pick, lang_weights, precision=lax.Precision.HIGHEST)[:, None, :]
        )
        padded_rows = jnp.pad(
            with_lang * live_rows, ((0, 0), (convolution_reach, convolution_reach), (0, 0))
        )
        convolution_sum = kernel_bias
        for index_of_tap in range(CONV_TAPS):
            convolution_sum = (
                convolution_sum
                + kernel_taps[index_of_tap]
                * padded_rows[
                    :, index_of_tap * CONV_DILATION : index_of_tap * CONV_DILATION + slots
                ]
            )
        return with_lang + convolution_sum

    def own(a):
        return lax.dynamic_slice_in_dim(a, mp * rows, rows, 1).reshape(own_rows, a.shape[2])

    tok_in = tokens.astype(f32).reshape(page_count, slots, width)
    first_pages, embed_back = jax.vjp(embed, tok_in, lang_table, convolution_weight, conv_b)
    first_own = own(first_pages)
    first_own_low = first_own.astype(bf16)
    first_keys = first_pages[:, :KEYS].astype(bf16).reshape(page_count * KEYS, width)
    table_t = jnp.transpose(bias_table)
    tab = jnp.stack([
        jnp.pad(t, ((0, 0), (0, LANES - t.shape[1])))
        for t in (table_t[:, :NB1], table_t[:, NB1 : NB1 + NB2], table_t[:, NB1 + NB2 :])
    ])
    tab = turned(tab.reshape(3, n_mp, heads_here, LANES), 1)

    blocks = [halves]
    bins = []
    held = ()
    for j in range(n_mp):
        one, two = blocks[j]
        bits = jnp.concatenate([one[2 * cols :], two[2 * cols :]], axis=0).reshape(-1)
        bits = bits[: 3 * (units + 2 * cols)].reshape(3, -1).astype(f32)
        bits = bits[0] + (bits[1] + bits[2])
        bins.append(bits[:units])
        held = attn_fwd(
            j, n_mp, page_len, first_own_low, first_keys, one, two, bits[units:].reshape(2, cols),
            rel_pos, rel_x, rel_y, tab[:, j], held,
        )
        if j == 0:
            held, moved = lax.optimization_barrier((held, moved))
            if paired:
                mate = [(i, i ^ 1) for i in range(n_dp)]
                others = [lax.ppermute(m, "dp", mate) for m in moved]
                blocks += [
                    (jnp.where(odd == 0, m, o), jnp.where(odd == 0, o, m))
                    for m, o in zip(moved, others)
                ]
            else:
                blocks += [(m[0], m[1]) for m in moved]
    mixed_low, probs, queries, key_rows, value_rows = held
    wos = [b[1][cols : 2 * cols] for b in blocks]
    bin_all = turned(jnp.stack(bins))
    attn_sum = 0.0
    for j in range(n_mp):
        attn_sum = attn_sum + dot_nn(mixed_low[j], wos[j]).astype(bf16).astype(f32)
    resid_one = first_own + attn_sum + b_out
    hidden_one, norm_one_back = jax.vjp(layer_norm, resid_one, ln1_gain, ln1_bias)
    hidden_low = hidden_one.astype(bf16)
    ffn_sum = 0.0
    acts = []
    for g in range(n_mp):
        pre_act = dot_nn(hidden_low, in_all[g]) + bin_all[g]
        activation, gelu_back = jax.vjp(exact_gelu, pre_act)
        activ_low = activation.astype(bf16)
        acts.append((activ_low, gelu_back))
        ffn_sum = ffn_sum + dot_nn(activ_low, down_all[g]).astype(bf16).astype(f32)
    resid_two = hidden_one + ffn_sum + b_down
    result, norm_two_back = jax.vjp(layer_norm, resid_two, ln2_gain, ln2_bias)

    def sent(a):
        return [a] + [shift(a, s) for s in range(1, n_mp)]

    def laid(line):
        line = turned(jnp.stack(line)).reshape(n_mp, page_count, rows, width)
        return jnp.transpose(line, (1, 0, 2, 3)).reshape(page_count * slots, width)

    out_line = sent(result.astype(bf16))

    cot_own = own(cotangent.reshape(page_count, slots, width)).astype(f32)
    grad_two, d_ln2_gain, d_ln2_bias = norm_two_back(cot_own)
    d_b_down = jnp.sum(grad_two, axis=0)
    grad_ffn = grad_two.astype(bf16)
    grad_hidden = grad_two
    d_in = []
    d_down = []
    d_bin = []
    for g in range(n_mp):
        activ_low, gelu_back = acts[g]
        d_down.append(dot_tn(activ_low, grad_ffn).astype(bf16))
        grad_pre = gelu_back(dot_nt(grad_ffn, down_all[g]))[0].astype(bf16)
        d_in.append(dot_tn(hidden_low, grad_pre).astype(bf16))
        d_bin.append(jnp.sum(grad_pre.astype(f32), axis=0))
        grad_hidden = grad_hidden + dot_nt(grad_pre, in_all[g])
    grad_one, d_ln1_gain, d_ln1_bias = norm_one_back(grad_hidden)
    d_b_out = jnp.sum(grad_one, axis=0)
    grad_attn = grad_one.astype(bf16)
    grad_mixed = jnp.stack([dot_nt(grad_attn, w_o).astype(bf16) for w_o in wos])

    ffn_parts = jnp.stack(d_in + d_down)
    ffn_parts, grad_mixed = lax.optimization_barrier((ffn_parts, grad_mixed))
    ffn_parts = lax.psum_scatter(ffn_parts, "dp", scatter_dimension=1, tiled=True)
    grads = attn_bwd(
        queries, key_rows, value_rows, grad_mixed, probs, rel_pos, rel_x, rel_y
    )
    grads, out_line = lax.optimization_barrier((grads, out_line))
    d_queries, d_keys, d_values, table_part = grads
    out = laid(out_line)
    dk_flat = d_keys.reshape(n_mp, page_count * KEYS, cols)
    dv_flat = d_values.reshape(n_mp, page_count * KEYS, cols)
    attn_parts = []
    for j in range(n_mp):
        attn_parts += [
            dot_tn(d_queries[j], first_own_low).astype(bf16),
            dot_tn(dk_flat[j], first_keys).astype(bf16),
            dot_tn(dv_flat[j], first_keys).astype(bf16),
            dot_tn(mixed_low[j], grad_attn).astype(bf16),
        ]
    attn_parts = jnp.stack(attn_parts)
    attn_parts, dk_flat, dv_flat, d_queries = lax.optimization_barrier(
        (attn_parts, dk_flat, dv_flat, d_queries)
    )
    attn_parts, ffn_parts = lax.optimization_barrier((attn_parts, ffn_parts))
    attn_parts = lax.psum_scatter(attn_parts, "dp", scatter_dimension=1, tiled=True)

    def to_owner(parts):
        total = lax.dynamic_index_in_dim(parts, mp, 0, keepdims=False).astype(f32)
        for s in range(1, n_mp):
            sent = lax.dynamic_index_in_dim(parts, (mp + s) % n_mp, 0, keepdims=False)
            total = total + shift(sent, s).astype(f32)
        return total.astype(bf16)

    ffn_parts = ffn_parts.reshape(2, n_mp, step, units)
    ffn_shares = to_owner(jnp.transpose(ffn_parts, (1, 0, 2, 3)))
    attn_shares = to_owner(turned(attn_parts.reshape(n_mp, 4, cols // n_dp, width)))
    own_part = grad_one
    key_part = 0.0
    for j in range(n_mp):
        w_q, w_k, w_v = blocks[j][0][:cols], blocks[j][0][cols : 2 * cols], blocks[j][1][:cols]
        own_part = own_part + dot_nn(d_queries[j], w_q)
        key_part = key_part + dot_nn(dk_flat[j], w_k) + dot_nn(dv_flat[j], w_v)
    own_part = own_part.reshape(page_count, rows, width)
    key_part = key_part.reshape(page_count, KEYS, width)
    grad_first = jnp.pad(key_part, ((0, 0), (0, slots - KEYS), (0, 0)))
    grad_first = lax.dynamic_update_slice_in_dim(
        grad_first,
        lax.dynamic_slice_in_dim(grad_first, mp * rows, rows, 1) + own_part,
        mp * rows,
        1,
    )
    d_tokens, d_lang_table, d_conv_w, d_conv_b = embed_back(grad_first)
    d_tokens = d_tokens.astype(bf16).reshape(page_count, n_mp, rows, width)
    d_tokens, ffn_shares = lax.optimization_barrier((d_tokens, ffn_shares))
    d_tokens = to_owner(jnp.transpose(d_tokens, (1, 0, 2, 3))).reshape(own_rows, width)
    d_tokens = laid(sent(d_tokens))

    ffn_shares = ffn_shares.reshape(-1, width)
    split = ffn_shares.shape[0]
    shares = jnp.concatenate([ffn_shares, attn_shares.reshape(-1, width)], axis=0)
    shares = lax.all_gather(shares, "dp", axis=0, tiled=False)
    ffn_blocks = shares[:, :split].reshape(n_dp, 2, step, units)
    d_w_in, d_w_down = [ffn_blocks[:, t].reshape(width, units).astype(f32) for t in range(2)]
    attn_blocks = shares[:, split:].reshape(n_dp, 4, cols // n_dp, width)
    attn_blocks = jnp.transpose(attn_blocks, (1, 0, 2, 3)).reshape(4, cols, width).astype(f32)
    d_w_qkv = jnp.transpose(attn_blocks[:3], (2, 0, 1))
    d_w_out = attn_blocks[3]

    dq_sum = jnp.sum(d_queries.astype(f32), axis=1)
    dv_sum = jnp.sum(dv_flat.astype(f32), axis=1)
    table_part = turned(table_part.reshape(-1, n_mp, heads_here), 1)
    smalls = [
        d_lang_table, d_conv_w, d_conv_b, turned(dq_sum), turned(dv_sum), table_part, d_b_out,
        d_ln1_gain, d_ln1_bias, jnp.concatenate(d_bin), d_b_down, d_ln2_gain, d_ln2_bias,
    ]
    flat = jnp.concatenate([s.reshape(-1) for s in smalls])
    count = flat.size
    flat = jnp.pad(flat, (0, -count % (8 * LANES))).reshape(-1, LANES)
    for axis, size in (("mp", n_mp), ("dp", n_dp)):
        if size & (size - 1):
            flat = lax.psum(flat, axis)
            continue
        for bit in range(size.bit_length() - 1):
            flat = flat + lax.ppermute(flat, axis, [(i, i ^ (1 << bit)) for i in range(size)])
    flat = flat.reshape(-1)
    back = []
    start = 0
    for s in smalls:
        back.append(flat[start : start + s.size].reshape(s.shape))
        start += s.size
    (d_lang_table, d_conv_w, d_conv_b, dq_sum, dv_sum, d_bias_table, d_b_out, d_ln1_gain,
     d_ln1_bias, d_b_in, d_b_down, d_ln2_gain, d_ln2_bias) = back
    d_b_qv = jnp.stack([
        lax.dynamic_index_in_dim(dq_sum, mp, 0, keepdims=False),
        lax.dynamic_index_in_dim(dv_sum, mp, 0, keepdims=False),
    ])
    d_b_in = lax.dynamic_slice_in_dim(d_b_in, mp * units, units)
    return (
        out,
        d_tokens,
        d_lang_table, d_conv_w, d_conv_b, d_w_qkv, d_b_qv,
        d_bias_table.reshape(-1, n_mp * heads_here), d_w_out, d_b_out,
        d_ln1_gain, d_ln1_bias, d_w_in, d_b_in, d_w_down, d_b_down, d_ln2_gain, d_ln2_bias,
    )


def solution(mesh):
    in_specs = (
        P("dp", None), P("dp"), P("dp"),
        P("dp", "mp", None), P("dp", "mp", None), P("dp", "mp", None),
        P(), P(), P(), P(None, None, "mp"), P(None, "mp"), P(), P("mp", None),
        P(), P(), P(), P(None, "mp"), P("mp"), P("mp", None), P(), P(), P(), P("dp", None),
    )
    out_specs = (
        P("dp", None), P("dp", None), P(), P(), P(), P(None, None, "mp"), P(None, "mp"), P(),
        P("mp", None), P(), P(), P(), P(None, "mp"), P("mp"), P("mp", None), P(), P(), P(),
    )
    step = functools.partial(body, n_dp=mesh.shape["dp"], n_mp=mesh.shape["mp"])
    return jax.shard_map(step, mesh=mesh, in_specs=in_specs, out_specs=out_specs, check_vma=False)
```

```python
import functools
import math

import jax
import jax.numpy as jnp
from jax import lax
from jax.experimental import pallas as pl
from jax.experimental.pallas import tpu as pltpu
from jax.sharding import PartitionSpec as P


HD = 64
NB1 = 32
NB2 = 64
CONV_TAPS = 3
CONV_DILATION = 2
PAGE_MAX = 561
LANES = 128
KEYS = -(-PAGE_MAX // LANES) * LANES
CHUNK = 16

norm_eps = 1e-05
masked_score = -1000000000.0
bf16 = jnp.bfloat16
f32 = jnp.float32


def layer_norm(inputs, norm_gain, norm_shift):
    row_mean = jnp.mean(inputs, axis=-1, keepdims=True)
    centred = inputs - row_mean
    spread = jnp.mean(centred * centred, axis=-1, keepdims=True)
    return centred * lax.rsqrt(spread + norm_eps) * norm_gain + norm_shift


def exact_gelu(inputs):
    return inputs * (0.5 + 0.5 * lax.erf(inputs * 0.5 ** 0.5))


def gelu_slope(inputs):
    bell = jnp.exp(-0.5 * inputs * inputs) * (2.0 * math.pi) ** -0.5
    return 0.5 + 0.5 * lax.erf(inputs * 0.5 ** 0.5) + inputs * bell


def dot_nt(a, b):
    return lax.dot_general(a, b, (((1,), (1,)), ((), ())), preferred_element_type=f32)


def dot_nn(a, b):
    return lax.dot_general(a, b, (((1,), (0,)), ((), ())), preferred_element_type=f32)


def dot_tn(a, b):
    return lax.dot_general(a, b, (((0,), (0,)), ((), ())), preferred_element_type=f32)


def attn_fwd_kernel(len_ref, own_ref, all_ref, one_ref, two_ref, bias_ref, pos_ref, x_ref, y_ref,
                    tab_ref, *rest):
    mixed_ref, p_ref, q_ref, k_ref, v_ref, s_ref, pb_ref = rest[-7:]
    page = pl.program_id(0)
    rows, width = q_ref.shape[1:]
    length = len_ref[page]
    lane = lax.broadcasted_iota(jnp.int32, (rows, width), 1)
    q = (dot_nt(own_ref[...], one_ref[0:width, :]) + bias_ref[0:1, :]).astype(bf16)
    q_ref[0] = (q.astype(f32) * HD ** -0.5).astype(bf16)
    k_ref[0, 0] = dot_nt(all_ref[...], one_ref[width : 2 * width, :]).astype(bf16)
    v_ref[0, 0] = (dot_nt(all_ref[...], two_ref[0:width, :]) + bias_ref[1:2, :]).astype(bf16)
    q = q_ref[0]
    k = k_ref[0, 0]
    v = v_ref[0, 0]
    mixed = jnp.zeros((rows, width), f32)
    for sub in range(width // HD):
        mine = (lane >= sub * HD) & (lane < (sub + 1) * HD)
        s_ref[sub] = dot_nt(jnp.where(mine, q, jnp.zeros_like(q)), k)
        tabs = [
            jnp.broadcast_to(tab_ref[t, sub : sub + 1, :], (CHUNK, LANES)) for t in range(3)
        ]

        def chunk(c, carry, sub=sub, tabs=tabs):
            at = pl.ds(pl.multiple_of(c * CHUNK, CHUNK), CHUNK)
            pieces = []
            for b in range(KEYS // LANES):
                cols = slice(b * LANES, (b + 1) * LANES)
                bias = None
                for tab, ids in zip(tabs, (pos_ref, x_ref, y_ref)):
                    got = jnp.take_along_axis(
                        tab, ids[0, at, cols], axis=1, mode="promise_in_bounds"
                    )
                    bias = got if bias is None else bias + got
                col = lax.broadcasted_iota(jnp.int32, (CHUNK, LANES), 1) + b * LANES
                val = s_ref[sub, at, cols] + bias.astype(bf16).astype(f32)
                pieces.append(jnp.where(col < length, val, masked_score))
            top = functools.reduce(jnp.maximum, pieces)
            top = jnp.max(top, axis=1, keepdims=True)
            es = [jnp.exp(piece - top) for piece in pieces]
            total = jnp.sum(functools.reduce(jnp.add, es), axis=1, keepdims=True)
            inv = 1.0 / total
            for b, e in enumerate(es):
                cols = slice(b * LANES, (b + 1) * LANES)
                prob = e * inv
                p_ref[0, 0, sub, at, cols] = prob
                pb_ref[sub, at, cols] = prob.astype(bf16)
            return carry

        lax.fori_loop(0, rows // CHUNK, chunk, 0, unroll=True)
        mixed = jnp.where(mine, dot_nn(pb_ref[sub], v), mixed)
    mixed_ref[0] = mixed.astype(bf16)


def attn_bwd_kernel(q_ref, k_ref, v_ref, gm_ref, p_ref, pos_ref, x_ref, y_ref,
                    dq_ref, dk_ref, dv_ref, tab_ref, dp_ref, pb_ref, ds_ref, all_ref):
    page = pl.program_id(0)
    group = pl.program_id(1)
    rows, width = q_ref.shape[1:]
    heads = width // HD
    lane = lax.broadcasted_iota(jnp.int32, (rows, width), 1)
    q = q_ref[0]
    gm = gm_ref[0]
    k = k_ref[0, 0]
    v = v_ref[0, 0]
    dk = dv = None
    dq = jnp.zeros((rows, width), f32)
    for sub in range(heads):
        mine = (lane >= sub * HD) & (lane < (sub + 1) * HD)
        qm = jnp.where(mine, q, jnp.zeros_like(q))
        gmm = jnp.where(mine, gm, jnp.zeros_like(gm))
        dp_ref[sub] = dot_nt(gmm, v)
        base = (group * heads + sub) * rows

        def chunk(c, carry, sub=sub, base=base):
            at = pl.ds(pl.multiple_of(c * CHUNK, CHUNK), CHUNK)
            to = pl.ds(pl.multiple_of(base + c * CHUNK, CHUNK), CHUNK)
            ps = []
            dps = []
            acc = None
            for b in range(KEYS // LANES):
                cols = slice(b * LANES, (b + 1) * LANES)
                ps.append(p_ref[0, 0, sub, at, cols])
                dps.append(dp_ref[sub, at, cols])
                prod = ps[-1] * dps[-1]
                acc = prod if acc is None else acc + prod
            mean = jnp.sum(acc, axis=1, keepdims=True)
            for b in range(KEYS // LANES):
                cols = slice(b * LANES, (b + 1) * LANES)
                ds = (ps[b] * (dps[b] - mean)).astype(bf16)
                pb_ref[sub, at, cols] = ps[b].astype(bf16)
                ds_ref[sub, at, cols] = ds
                all_ref[b, to, :] = ds.astype(f32)
            return carry

        lax.fori_loop(0, rows // CHUNK, chunk, 0, unroll=True)
        dq = jnp.where(mine, dot_nn(ds_ref[sub], k), dq)
        dkh = dot_tn(ds_ref[sub], qm)
        dvh = dot_tn(pb_ref[sub], gmm)
        dk = dkh if dk is None else dk + dkh
        dv = dvh if dv is None else dv + dvh
    dq_ref[0] = (dq * HD ** -0.5).astype(bf16)
    dk_ref[0, 0] = dk.astype(bf16)
    dv_ref[0, 0] = dv.astype(bf16)

    @pl.when((page == 0) & (group == 0))
    def _():
        tab_ref[...] = jnp.zeros_like(tab_ref)

    @pl.when(group == pl.num_programs(1) - 1)
    def _():
        nheads = tab_ref.shape[1]

        def row(i, accs):
            g = jnp.concatenate(
                [all_ref[b, pl.ds(i, nheads, stride=rows), :] for b in range(KEYS // LANES)],
                axis=1,
            ).astype(bf16)
            new = []
            for acc, ids, count in zip(accs, (pos_ref, x_ref, y_ref), (NB1, NB2, NB2)):
                idr = ids[0, pl.ds(i, 1), :].astype(f32).astype(bf16)
                bucket = lax.broadcasted_iota(jnp.int32, (count, KEYS), 0).astype(f32).astype(bf16)
                hit = jnp.where(bucket == idr, jnp.ones((), bf16), jnp.zeros((), bf16))
                new.append(acc + dot_nt(hit, g))
            return tuple(new)

        accs = tuple(jnp.zeros((c, nheads), f32) for c in (NB1, NB2, NB2))
        accs = lax.fori_loop(0, rows, row, accs, unroll=4)
        tab_ref[0:NB1, :] += accs[0]
        tab_ref[NB1 : NB1 + NB2, :] += accs[1]
        tab_ref[NB1 + NB2 : NB1 + 2 * NB2, :] += accs[2]


def attn_fwd(group, groups, page_len, own_in, all_in, one, two, bias, pos, x, y, tab, held):
    pages, rows, _ = pos.shape
    width = bias.shape[1]
    depth = own_in.shape[1]
    heads = width // HD
    ids = pl.BlockSpec((1, rows, KEYS), lambda p, *_: (p, 0, 0))
    kv = pl.BlockSpec((1, 1, KEYS, width), lambda p, *_: (group, p, 0, 0))
    qs = pl.BlockSpec((1, rows, width), lambda p, *_: (group, p, 0))
    kv_all = jax.ShapeDtypeStruct((groups, pages, KEYS, width), bf16)
    q_all = jax.ShapeDtypeStruct((groups, pages * rows, width), bf16)
    carried = [pl.BlockSpec(memory_space=pl.ANY)] * len(held)
    elements = pages * rows * heads * KEYS
    return pl.pallas_call(
        attn_fwd_kernel,
        out_shape=(
            q_all,
            jax.ShapeDtypeStruct((groups, pages, heads, rows, KEYS), f32),
            q_all,
            kv_all,
            kv_all,
        ),
        grid_spec=pltpu.PrefetchScalarGridSpec(
            num_scalar_prefetch=1,
            grid=(pages,),
            in_specs=[
                pl.BlockSpec((rows, depth), lambda p, *_: (p, 0)),
                pl.BlockSpec((KEYS, depth), lambda p, *_: (p, 0)),
                pl.BlockSpec(one.shape, lambda p, *_: (0, 0)),
                pl.BlockSpec(two.shape, lambda p, *_: (0, 0)),
                pl.BlockSpec(bias.shape, lambda p, *_: (0, 0)),
                ids, ids, ids,
                pl.BlockSpec(tab.shape, lambda p, *_: (0, 0, 0)),
            ] + carried,
            out_specs=(
                qs,
                pl.BlockSpec((1, 1, heads, rows, KEYS), lambda p, *_: (group, p, 0, 0, 0)),
                qs, kv, kv,
            ),
            scratch_shapes=[
                pltpu.VMEM((heads, rows, KEYS), f32), pltpu.VMEM((heads, rows, KEYS), bf16)
            ],
        ),
        input_output_aliases={10 + i: i for i in range(len(held))},
        cost_estimate=pl.CostEstimate(
            flops=20000 * elements, transcendentals=elements, bytes_accessed=16 * elements
        ),
    )(page_len, own_in, all_in, one, two, bias, pos, x, y, tab, *held)


def attn_bwd(q, k, v, gm, p, pos, x, y):
    pages, rows, _ = pos.shape
    groups, _, width = q.shape
    heads = width // HD
    qs = pl.BlockSpec((1, rows, width), lambda p, g: (g, p, 0))
    ks = pl.BlockSpec((1, 1, KEYS, width), lambda p, g: (g, p, 0, 0))
    ids = pl.BlockSpec((1, rows, KEYS), lambda p, g: (p, 0, 0))
    ps = pl.BlockSpec((1, 1, heads, rows, KEYS), lambda p, g: (g, p, 0, 0, 0))
    kv = jax.ShapeDtypeStruct(k.shape, bf16)
    table = (NB1 + 2 * NB2, groups * heads)
    elements = pages * rows * groups * heads * KEYS
    return pl.pallas_call(
        attn_bwd_kernel,
        out_shape=(jax.ShapeDtypeStruct(q.shape, bf16), kv, kv, jax.ShapeDtypeStruct(table, f32)),
        grid=(pages, groups),
        in_specs=[qs, ks, ks, qs, ps, ids, ids, ids],
        out_specs=(qs, ks, ks, pl.BlockSpec(table, lambda p, g: (0, 0))),
        scratch_shapes=[
            pltpu.VMEM((heads, rows, KEYS), f32),
            pltpu.VMEM((heads, rows, KEYS), bf16),
            pltpu.VMEM((heads, rows, KEYS), bf16),
            pltpu.VMEM((KEYS // LANES, groups * heads * rows, LANES), f32),
        ],
        cost_estimate=pl.CostEstimate(
            flops=20000 * elements, transcendentals=elements, bytes_accessed=16 * elements
        ),
    )(q, k, v, gm, p, pos, x, y)


def body(tokens, lang, page_len, rel_pos, rel_x, rel_y, lang_table, convolution_weight, conv_b,
         w_qkv, b_qv, bias_table, w_out, b_out, ln1_gain, ln1_bias, w_in, b_in, w_down, b_down,
         ln2_gain, ln2_bias, cotangent, *, n_dp, n_mp):
    dp = lax.axis_index("dp")
    mp = lax.axis_index("mp")
    page_count = page_len.shape[0]
    rows = rel_pos.shape[1]
    slots = rel_pos.shape[2]
    width = tokens.shape[1]
    cols = w_qkv.shape[2]
    units = w_in.shape[1]
    own_rows = page_count * rows
    heads_here = cols // HD
    paired = n_dp % 2 == 0
    order = (mp - jnp.arange(n_mp)) % n_mp

    def turned(a, axis=0):
        return jnp.take(a, order, axis=axis, mode="clip")

    def shift(a, s):
        return lax.ppermute(a, "mp", [(i, (i + s) % n_mp) for i in range(n_mp)])

    step = width // n_dp
    unit_step = units // n_dp
    share = jnp.concatenate([
        lax.dynamic_slice_in_dim(w_in, dp * step, step, 0),
        lax.dynamic_slice_in_dim(w_down, dp * unit_step, unit_step, 0),
    ], axis=1)
    ffn_all = lax.all_gather(share, ("mp", "dp"), axis=0, tiled=True)
    ffn_all = ffn_all.reshape(n_mp, width, 2 * units)
    in_all = [ffn_all[g, :, :units] for g in range(n_mp)]
    down_all = [ffn_all[g, :, units:] for g in range(n_mp)]

    biases = jnp.concatenate([b_in, b_qv.reshape(-1)])
    thirds = []
    for _ in range(3):
        top = lax.reduce_precision(biases, 8, 7)
        thirds.append(top.astype(bf16))
        biases = biases - top
    thirds = jnp.concatenate(thirds)
    tail = -(-thirds.size // (16 * width)) * 16
    thirds = jnp.pad(thirds, (0, tail * width - thirds.size)).reshape(tail, width)
    qkv_t = jnp.transpose(w_qkv.reshape(width, 3 * cols))
    halves = [
        jnp.concatenate([qkv_t[: 2 * cols], thirds[: tail // 2]], axis=0),
        jnp.concatenate([qkv_t[2 * cols :], w_out, thirds[tail // 2 :]], axis=0),
    ]
    odd = dp % 2
    moving = jnp.where(odd == 0, halves[0], halves[1]) if paired else jnp.stack(halves)
    moving = shift(moving, 1)

    slot_index = lax.broadcasted_iota(jnp.int32, (page_count, slots), 1)
    live_rows = (slot_index < page_len[:, None]).astype(f32)[:, :, None]
    languages = lax.broadcasted_iota(jnp.int32, (1, lang_table.shape[0]), 1)
    lang_pick = (lang[:, None] == languages).astype(f32)
    convolution_reach = CONV_TAPS // 2 * CONV_DILATION

    def embed(tok_in, lang_weights, kernel_taps, kernel_bias):
        with_lang = (
            tok_in + jnp.dot(lang_pick, lang_weights, precision=lax.Precision.HIGHEST)[:, None, :]
        )
        padded_rows = jnp.pad(
            with_lang * live_rows, ((0, 0), (convolution_reach, convolution_reach), (0, 0))
        )
        convolution_sum = kernel_bias
        for index_of_tap in range(CONV_TAPS):
            convolution_sum = (
                convolution_sum
                + kernel_taps[index_of_tap]
                * padded_rows[
                    :, index_of_tap * CONV_DILATION : index_of_tap * CONV_DILATION + slots
                ]
            )
        return with_lang + convolution_sum

    def own(a):
        return lax.dynamic_slice_in_dim(a, mp * rows, rows, 1).reshape(own_rows, a.shape[2])

    tok_in = tokens.astype(f32).reshape(page_count, slots, width)
    first_pages, embed_back = jax.vjp(embed, tok_in, lang_table, convolution_weight, conv_b)
    first_own = own(first_pages)
    first_own_low = first_own.astype(bf16)
    first_keys = first_pages[:, :KEYS].astype(bf16).reshape(page_count * KEYS, width)
    table_t = jnp.transpose(bias_table)
    tab = jnp.stack([
        jnp.pad(t, ((0, 0), (0, LANES - t.shape[1])))
        for t in (table_t[:, :NB1], table_t[:, NB1 : NB1 + NB2], table_t[:, NB1 + NB2 :])
    ])
    tab = turned(tab.reshape(3, n_mp, heads_here, LANES), 1)

    first_own_low, moving = lax.optimization_barrier((first_own_low, moving))
    blocks = [halves]
    bins = []
    held = ()
    for j in range(n_mp):
        one, two = blocks[j]
        bits = jnp.concatenate([one[2 * cols :], two[2 * cols :]], axis=0).reshape(-1)
        bits = bits[: 3 * (units + 2 * cols)].reshape(3, -1).astype(f32)
        bits = bits[0] + (bits[1] + bits[2])
        bins.append(bits[:units])
        held = attn_fwd(
            j, n_mp, page_len, first_own_low, first_keys, one, two, bits[units:].reshape(2, cols),
            rel_pos, rel_x, rel_y, tab[:, j], held,
        )
        if j + 1 == n_mp:
            break
        after = shift(moving, 1) if j + 2 < n_mp else moving
        if paired:
            other = lax.ppermute(moving, "dp", [(i, i ^ 1) for i in range(n_dp)])
            held, after, other = lax.optimization_barrier((held, after, other))
            blocks.append(
                (jnp.where(odd == 0, moving, other), jnp.where(odd == 0, other, moving))
            )
        else:
            held, after = lax.optimization_barrier((held, after))
            blocks.append((moving[0], moving[1]))
        moving = after
    mixed_low, probs, queries, key_rows, value_rows = held
    wos = [b[1][cols : 2 * cols] for b in blocks]
    bin_all = turned(jnp.stack(bins))
    attn_sum = 0.0
    for j in range(n_mp):
        attn_sum = attn_sum + dot_nn(mixed_low[j], wos[j]).astype(bf16).astype(f32)
    resid_one = first_own + attn_sum + b_out
    hidden_one, norm_one_back = jax.vjp(layer_norm, resid_one, ln1_gain, ln1_bias)
    hidden_low = hidden_one.astype(bf16)
    ffn_sum = 0.0
    acts = []
    for g in range(n_mp):
        pre_act = dot_nn(hidden_low, in_all[g]) + bin_all[g]
        activ_low = exact_gelu(pre_act).astype(bf16)
        acts.append((activ_low, gelu_slope(pre_act)))
        ffn_sum = ffn_sum + dot_nn(activ_low, down_all[g]).astype(bf16).astype(f32)
    resid_two = hidden_one + ffn_sum + b_down
    result, norm_two_back = jax.vjp(layer_norm, resid_two, ln2_gain, ln2_bias)

    def sent(a):
        return [a] + [shift(a, s) for s in range(1, n_mp)]

    def laid(line):
        whole = jnp.zeros((page_count, slots, width), bf16)
        for j, piece in enumerate(line):
            at = (mp - j) % n_mp * rows
            whole = lax.dynamic_update_slice_in_dim(
                whole, piece.reshape(page_count, rows, width), at, 1
            )
        return whole.reshape(page_count * slots, width)

    out_line = sent(result.astype(bf16))

    cot_own = own(cotangent.reshape(page_count, slots, width)).astype(f32)
    grad_two, d_ln2_gain, d_ln2_bias = norm_two_back(cot_own)
    d_b_down = jnp.sum(grad_two, axis=0)
    grad_ffn = grad_two.astype(bf16)
    grad_hidden = grad_two
    d_in = []
    d_down = []
    d_bin = []
    for g in range(n_mp):
        activ_low, slope = acts[g]
        d_down.append(dot_tn(activ_low, grad_ffn).astype(bf16))
        grad_pre = (slope * dot_nt(grad_ffn, down_all[g])).astype(bf16)
        d_in.append(dot_tn(hidden_low, grad_pre).astype(bf16))
        d_bin.append(jnp.sum(grad_pre.astype(f32), axis=0))
        grad_hidden = grad_hidden + dot_nt(grad_pre, in_all[g])
    grad_one, d_ln1_gain, d_ln1_bias = norm_one_back(grad_hidden)
    d_b_out = jnp.sum(grad_one, axis=0)
    grad_attn = grad_one.astype(bf16)
    grad_mixed = jnp.stack([dot_nt(grad_attn, w_o).astype(bf16) for w_o in wos])

    ffn_parts = jnp.stack(d_in + d_down)
    ffn_parts, grad_mixed = lax.optimization_barrier((ffn_parts, grad_mixed))
    ffn_parts = lax.psum_scatter(ffn_parts, "dp", scatter_dimension=1, tiled=True)
    grads = attn_bwd(
        queries, key_rows, value_rows, grad_mixed, probs, rel_pos, rel_x, rel_y
    )
    grads, out_line = lax.optimization_barrier((grads, out_line))
    d_queries, d_keys, d_values, table_part = grads
    out = laid(out_line)
    dk_flat = d_keys.reshape(n_mp, page_count * KEYS, cols)
    dv_flat = d_values.reshape(n_mp, page_count * KEYS, cols)

    def to_owners(parts):
        return [
            shift(lax.dynamic_index_in_dim(parts, (mp + s) % n_mp, 0, keepdims=False), s)
            if s else lax.dynamic_index_in_dim(parts, mp, 0, keepdims=False)
            for s in range(n_mp)
        ]

    def owner_sum(terms):
        return sum(t.astype(f32) for t in terms).astype(bf16)

    own_part = grad_one
    key_part = 0.0
    for j in range(n_mp):
        w_q, w_k, w_v = blocks[j][0][:cols], blocks[j][0][cols : 2 * cols], blocks[j][1][:cols]
        own_part = own_part + dot_nn(d_queries[j], w_q)
        key_part = key_part + dot_nn(dk_flat[j], w_k) + dot_nn(dv_flat[j], w_v)
    own_part = own_part.reshape(page_count, rows, width)
    key_part = key_part.reshape(page_count, KEYS, width)
    grad_first = jnp.pad(key_part, ((0, 0), (0, slots - KEYS), (0, 0)))
    grad_first = lax.dynamic_update_slice_in_dim(
        grad_first,
        lax.dynamic_slice_in_dim(grad_first, mp * rows, rows, 1) + own_part,
        mp * rows,
        1,
    )
    d_tokens, d_lang_table, d_conv_w, d_conv_b = embed_back(grad_first)
    d_tokens = d_tokens.astype(bf16).reshape(page_count, n_mp, rows, width)
    d_tokens = jnp.transpose(d_tokens, (1, 0, 2, 3))
    d_tokens, dk_flat, dv_flat, d_queries = lax.optimization_barrier(
        (d_tokens, dk_flat, dv_flat, d_queries)
    )
    d_tokens = to_owners(d_tokens)

    def by_group(left, right):
        return lax.dot_general(
            left, right, (((1,), (0,)), ((), ())), preferred_element_type=f32
        ).astype(bf16)

    attn_parts = jnp.concatenate([
        by_group(d_queries, first_own_low),
        by_group(dk_flat, first_keys),
        by_group(dv_flat, first_keys),
        by_group(mixed_low, grad_attn),
    ], axis=0)
    attn_parts, ffn_parts = lax.optimization_barrier((attn_parts, ffn_parts))
    attn_parts = lax.psum_scatter(attn_parts, "dp", scatter_dimension=1, tiled=True)
    ffn_parts = ffn_parts.reshape(2, n_mp, step, units)
    ffn_shares = owner_sum(to_owners(jnp.transpose(ffn_parts, (1, 0, 2, 3))))
    dq_sum = jnp.sum(d_queries.astype(f32), axis=1)
    dv_sum = jnp.sum(dv_flat.astype(f32), axis=1)
    table_part = turned(table_part.reshape(-1, n_mp, heads_here), 1)
    smalls = [
        d_lang_table, d_conv_w, d_conv_b, turned(dq_sum), turned(dv_sum), table_part, d_b_out,
        d_ln1_gain, d_ln1_bias, jnp.concatenate(d_bin), d_b_down, d_ln2_gain, d_ln2_bias,
    ]
    flat = jnp.concatenate([s.reshape(-1) for s in smalls])
    count = flat.size
    flat = jnp.pad(flat, (0, -count % (8 * LANES))).reshape(-1, LANES)
    for axis, size in (("mp", n_mp), ("dp", n_dp)):
        if size & (size - 1):
            flat = lax.psum(flat, axis)
            continue
        for bit in range(size.bit_length() - 1):
            flat = flat + lax.ppermute(flat, axis, [(i, i ^ (1 << bit)) for i in range(size)])
    d_tokens, flat, ffn_shares, attn_parts = lax.optimization_barrier(
        (d_tokens, flat, ffn_shares, attn_parts)
    )
    lines = sent(owner_sum(d_tokens).reshape(own_rows, width))
    attn_parts = turned(attn_parts.reshape(4, n_mp, cols // n_dp, width), 1)
    attn_shares = owner_sum(to_owners(jnp.transpose(attn_parts, (1, 0, 2, 3))))
    ffn_shares = ffn_shares.reshape(-1, width)
    split = ffn_shares.shape[0]
    shares = jnp.concatenate([ffn_shares, attn_shares.reshape(-1, width)], axis=0)
    shares = lax.all_gather(shares, "dp", axis=0, tiled=False)
    ffn_blocks = shares[:, :split].reshape(n_dp, 2, step, units)
    d_w_in, d_w_down = [ffn_blocks[:, t].reshape(width, units).astype(f32) for t in range(2)]
    attn_blocks = shares[:, split:].reshape(n_dp, 4, cols // n_dp, width)
    attn_blocks = jnp.transpose(attn_blocks, (1, 0, 2, 3)).reshape(4, cols, width).astype(f32)
    d_w_qkv = jnp.transpose(attn_blocks[:3], (2, 0, 1))
    d_w_out = attn_blocks[3]

    d_tokens = laid(lines)
    flat = flat.reshape(-1)
    back = []
    start = 0
    for s in smalls:
        back.append(flat[start : start + s.size].reshape(s.shape))
        start += s.size
    (d_lang_table, d_conv_w, d_conv_b, dq_sum, dv_sum, d_bias_table, d_b_out, d_ln1_gain,
     d_ln1_bias, d_b_in, d_b_down, d_ln2_gain, d_ln2_bias) = back
    d_b_qv = jnp.stack([
        lax.dynamic_index_in_dim(dq_sum, mp, 0, keepdims=False),
        lax.dynamic_index_in_dim(dv_sum, mp, 0, keepdims=False),
    ])
    d_b_in = lax.dynamic_slice_in_dim(d_b_in, mp * units, units)
    return (
        out,
        d_tokens,
        d_lang_table, d_conv_w, d_conv_b, d_w_qkv, d_b_qv,
        d_bias_table.reshape(-1, n_mp * heads_here), d_w_out, d_b_out,
        d_ln1_gain, d_ln1_bias, d_w_in, d_b_in, d_w_down, d_b_down, d_ln2_gain, d_ln2_bias,
    )


def solution(mesh):
    in_specs = (
        P("dp", None), P("dp"), P("dp"),
        P("dp", "mp", None), P("dp", "mp", None), P("dp", "mp", None),
        P(), P(), P(), P(None, None, "mp"), P(None, "mp"), P(), P("mp", None),
        P(), P(), P(), P(None, "mp"), P("mp"), P("mp", None), P(), P(), P(), P("dp", None),
    )
    out_specs = (
        P("dp", None), P("dp", None), P(), P(), P(), P(None, None, "mp"), P(None, "mp"), P(),
        P("mp", None), P(), P(), P(), P(None, "mp"), P("mp"), P("mp", None), P(), P(), P(),
    )

    def step(*args):
        return body(*args, n_dp=mesh.shape["dp"], n_mp=mesh.shape["mp"])

    return jax.shard_map(
        step, mesh=mesh, in_specs=in_specs, out_specs=out_specs, check_vma=False
    )
```
